32 devices in a mesh: energy: 8 (over z, y), wire: 4 (over x, core).
Axes of the slice: x: 2, y: 2, z: 4, core: 2. Of those that a mesh axis runs over, the one named last changes fastest.
Arguments:
- green_ret: float32 [2, 8, 8, 128, 128], P(None, 'energy', 'wire'), may hold values from -0.375 to 0.375
- coupling: float32 [2, 8, 128, 128], P(None, 'wire'), may hold values from -0.375 to 0.375
- sigma_less_in: float32 [2, 8, 8, 4096], P(None, 'energy', 'wire'), may hold values from -3 to 3
- sigma_greater_in: float32 [2, 8, 8, 4096], P(None, 'energy', 'wire'), may hold values from -3 to 3
- screened_less: float32 [2, 8, 8, 4096], P(None, 'energy', 'wire'), may hold values from -6 to 6
- screened_greater: float32 [2, 8, 8, 4096], P(None, 'energy', 'wire'), may hold values from -6 to 6
- pattern: int32 [8, 4096], P('wire'), may hold values from 0 to 16383, as said below
- counts: int32 [8], P('wire'), may hold values from 1024 to 4096, as said below
Outputs:
- green_less: float32 [2, 8, 8, 128, 128], P(None, 'energy', 'wire')
- green_greater: float32 [2, 8, 8, 128, 128], P(None, 'energy', 'wire')
- sigma_less: float32 [2, 8, 8, 4096], P(None, 'energy', 'wire')
- sigma_greater: float32 [2, 8, 8, 4096], P(None, 'energy', 'wire')
The draws below stay inside these ranges and needn't reach their ends.
Inputs may be any that keep to these rules, and one draw needn't show every extreme that they name: `pattern`: within each block the 4096 positions are distinct; positions 0 and 16383 both occur in some block. `counts`: some block has all 4096 slots live and some block only 1024.
All inputs are finite; a program needn't handle non-finite values.
Results may differ from the reference program's by a relative error of at most 0.00016.
Values sent between devices are 32-bit elements; how exact they have to be, the bound alone decides.
A program may use at most 64 MiB of HBM per device.

```python
import jax
import jax.numpy as jnp
from jax import lax

B = 128
NZ = 4096
ENERGIES = 8
NB = 8


def draw_pattern(key, part):
    keys = jax.random.split(key, NB)

    def one_block(block_key):
        return jax.random.permutation(block_key, B * B)[:NZ]
    drawn = jax.vmap(one_block)(keys)
    inner = jax.random.permutation(jax.random.fold_in(key, 7), B * B - 2)[:NZ - 2] + 1
    with_ends = jnp.concatenate([inner, jnp.array([0, B * B - 1])])
    with_ends = jax.random.permutation(jax.random.fold_in(key, 11), with_ends)
    chosen = jax.random.randint(jax.random.fold_in(key, 13), (), 0, NB)
    rows = jnp.arange(NB)[:, None]
    return jnp.where(rows == chosen, with_ends[None, :], drawn).astype(jnp.int32)


def draw_counts(key, part):
    base = jax.random.randint(key, (NB,), NZ // 4, NZ + 1)
    fullest = jax.random.randint(jax.random.fold_in(key, 3), (), 0, NB)
    offset = jax.random.randint(jax.random.fold_in(key, 5), (), 1, NB)
    emptiest = (fullest + offset) % NB
    base = base.at[fullest].set(NZ).at[emptiest].set(NZ // 4)
    return base.astype(jnp.int32)


def steps_of(key, shape, cuts, smallest, largest):
    loudness = 1.0
    for position, blocks in cuts:
        heights = jax.random.uniform(jax.random.fold_in(jax.random.fold_in(key, 6), position), (blocks,), jnp.float32, smallest / len(cuts), largest / len(cuts))
        loudness = loudness * jnp.repeat(jnp.exp(heights), shape[position] // blocks).reshape((-1,) + (1,) * (len(shape) - 1 - position))
    return loudness


def normal_values(key, shape, spread, most, cuts=(), held_as=jnp.bfloat16):
    result = jax.random.normal(key, shape, jnp.float32) * spread
    if len(cuts) > 0:
        result = steps_of(key, shape, cuts, -0.22, 0.18) * result
    return jnp.clip(result, min=-most, max=most).astype(held_as)


def setup_inputs(seed: int = 0) -> dict:
    splits = jax.random.split(jax.random.key(seed), 9)
    green_ret = normal_values(splits[0], (2, ENERGIES, NB, B, B), (2 * B) ** -0.5, 0.375, ((1, 8), (2, 4)), jnp.float32)
    coupling = normal_values(splits[1], (2, NB, B, B), (2 * B + B // 16) ** -0.5, 0.375, ((1, 4),), jnp.float32)
    sigma_less_in = normal_values(splits[2], (2, ENERGIES, NB, NZ), 0.5, 3.0, ((1, 8), (2, 4)), jnp.float32)
    sigma_greater_in = normal_values(splits[3], (2, ENERGIES, NB, NZ), 0.5, 3.0, ((1, 8), (2, 4)), jnp.float32)
    screened_less = normal_values(splits[4], (2, ENERGIES, NB, NZ), 1.0, 6.0, ((1, 8), (2, 4)), jnp.float32)
    screened_greater = normal_values(splits[5], (2, ENERGIES, NB, NZ), 1.0, 6.0, ((1, 8), (2, 4)), jnp.float32)
    pattern = draw_pattern(jax.random.fold_in(splits[8], 71), 0)
    counts = draw_counts(jax.random.fold_in(splits[8], 71), 0)
    return {"green_ret": green_ret, "coupling": coupling, "sigma_less_in": sigma_less_in, "sigma_greater_in": sigma_greater_in, "screened_less": screened_less, "screened_greater": screened_greater, "pattern": pattern, "counts": counts}


exact_precision = lax.Precision.HIGHEST


def highest_dot(left, right):
    return jnp.matmul(left, right, precision=exact_precision)


def complex_product(left, right):
    real_part = highest_dot(left[0], right[0]) - highest_dot(left[1], right[1])
    imag_part = highest_dot(left[0], right[1]) + highest_dot(left[1], right[0])
    return jnp.stack([real_part, imag_part])


def adjoint(matrix):
    return jnp.stack([jnp.swapaxes(matrix[0], -1, -2), -jnp.swapaxes(matrix[1], -1, -2)])


def sandwich(outer, inner):
    return complex_product(complex_product(outer, inner), adjoint(outer))


def block_dense(values, positions, mask):
    flat = jnp.zeros(values.shape[:2] + (B * B,), jnp.float32)
    flat = flat.at[:, :, positions].add(values * mask)
    return flat.reshape(values.shape[:2] + (B, B))


def convolve(green_slots, screen_slots):
    count = green_slots.shape[1]
    padded = jnp.concatenate([jnp.zeros_like(green_slots), green_slots], axis=1)

    def add_shift(shift, total):
        shift = shift.astype(jnp.int32)
        moved = lax.dynamic_slice_in_dim(padded, jnp.int32(count) - shift, count, 1)
        weight = lax.dynamic_slice_in_dim(screen_slots, shift, 1, 1)
        real_part = moved[0] * weight[0] - moved[1] * weight[1]
        imag_part = moved[0] * weight[1] + moved[1] * weight[0]
        return total + jnp.stack([real_part, imag_part])

    total = lax.fori_loop(0, count, add_shift, jnp.zeros_like(green_slots))
    scale = count ** -0.5
    return jnp.stack([-scale * total[1], scale * total[0]])


def reference(green_ret, coupling, sigma_less_in, sigma_greater_in, screened_less, screened_greater, pattern, counts):
    slots = jnp.arange(pattern.shape[1], dtype=jnp.int32)
    live = (slots[None, :] < counts[:, None]).astype(jnp.float32)
    zeros = jnp.zeros((2, green_ret.shape[1], B, B), jnp.float32)

    def advance(carry, inputs):
        less_state, greater_state = carry
        green_block, couple_block, less_in, greater_in, positions, mask = inputs
        multiplier = complex_product(green_block, couple_block[:, None])
        source_less = sandwich(green_block, block_dense(less_in, positions, mask))
        source_greater = sandwich(green_block, block_dense(greater_in, positions, mask))
        less_state = source_less + sandwich(multiplier, less_state)
        greater_state = source_greater + sandwich(multiplier, greater_state)
        return (less_state, greater_state), (less_state, greater_state)

    inputs = (jnp.moveaxis(green_ret, 2, 0), jnp.moveaxis(coupling, 1, 0), jnp.moveaxis(sigma_less_in, 2, 0),
              jnp.moveaxis(sigma_greater_in, 2, 0), pattern, live)
    finals, states = lax.scan(advance, (zeros, zeros), inputs)
    green_less = jnp.moveaxis(states[0], 0, 2)
    green_greater = jnp.moveaxis(states[1], 0, 2)
    rows = jnp.arange(pattern.shape[0], dtype=jnp.int32)[:, None]
    flat_less = green_less.reshape(green_less.shape[:3] + (B * B,))
    flat_greater = green_greater.reshape(green_greater.shape[:3] + (B * B,))
    less_slots = flat_less[:, :, rows, pattern] * live
    greater_slots = flat_greater[:, :, rows, pattern] * live
    sigma_less = convolve(less_slots, screened_less)
    sigma_greater = convolve(greater_slots, screened_greater)
    return green_less, green_greater, sigma_less, sigma_greater
```

```python
import functools

import jax
import jax.numpy as jnp
from jax import lax
from jax.experimental import pallas as pl
from jax.experimental.pallas import tpu as pltpu
from jax.sharding import PartitionSpec as P

MESH = pl.DeviceIdType.MESH
F32 = jnp.float32
BF16 = jnp.bfloat16


def split(x):
    hi = x.astype(BF16)
    lo = (x - hi.astype(F32)).astype(BF16)
    return hi, lo


def dot_nn(a, b):
    return lax.dot_general(a, b, (((1,), (0,)), ((), ())), preferred_element_type=F32)


def dot_nt(a, b):
    return lax.dot_general(a, b, (((1,), (1,)), ((), ())), preferred_element_type=F32)


def dot3(dot, a, b):
    return dot(a[0], b[0]) + (dot(a[1], b[0]) + dot(a[0], b[1]))


def full_one(row):
    n = row.shape[1] // 2
    re, im = row[:, :n], row[:, n:]
    return jnp.concatenate(
        [jnp.concatenate([re, im], axis=1), jnp.concatenate([-im, re], axis=1)], axis=0
    )


def full(row):
    return full_one(row[0]), full_one(row[1])


def sandwich(row, square, state):
    n = row[0].shape[0]
    stacked = state.reshape(2 * n, 2 * n)
    right = dot3(dot_nt, split(stacked), square)
    hi, lo = split(right)
    wide = tuple(
        jnp.concatenate([full_one(x[:n]), full_one(x[n:])], axis=1) for x in (hi, lo)
    )
    out = dot3(dot_nn, row, wide)
    return out[:, : 2 * n], out[:, 2 * n :]


def kernel(
    n_energy, n_wire,
    g_hbm, c_hbm, sl_hbm, sg_hbm, wl_hbm, wg_hbm, pat_hbm, cnt_ref,
    gl_hbm, gg_hbm, ol_ref, og_ref,
    g, c, sl, sg, wl, wg, pat,
    acc, st, pin, lhs, send_w, recv_w, send_g, recv_g, send_s, recv_s,
    in_sem, out_sem, ring_send, ring_recv, sw_sem, rw_sem, sg_sem, rg_sem, ss_sem, rs_sem,
):
    e = lax.axis_index("energy")
    w = lax.axis_index("wire")
    blocks = g.shape[1]
    n = g.shape[2]
    slots = pat.shape[1]
    part = slots // n_energy
    rows = 4 * blocks

    barrier = pltpu.get_barrier_semaphore()

    def greet(d, carry):
        peer = lax.rem(e + d, n_energy)
        pl.semaphore_signal(barrier, inc=1, device_id={"energy": peer}, device_id_type=MESH)
        return carry

    lax.fori_loop(1, n_energy, greet, 0)

    @pl.when(w > 0)
    def _():
        pl.semaphore_signal(barrier, inc=1, device_id={"wire": w - 1}, device_id_type=MESH)

    @pl.when(w < n_wire - 1)
    def _():
        pl.semaphore_signal(barrier, inc=1, device_id={"wire": w + 1}, device_id_type=MESH)

    pairs = [(pat_hbm, pat), (sl_hbm, sl), (sg_hbm, sg), (wl_hbm, wl), (wg_hbm, wg),
             (g_hbm, g), (c_hbm, c)]
    loads = [pltpu.make_async_copy(s, d, in_sem.at[i]) for i, (s, d) in enumerate(pairs)]
    for copy in loads:
        copy.start()

    loads[3].wait()
    loads[4].wait()
    for t in range(n_energy):
        for p in range(2):
            for k, ref in enumerate((wl, wg)):
                for b in range(blocks):
                    row = p * 2 * blocks + k * blocks + b
                    send_w[t, row : row + 1, :] = ref[p, b : b + 1, t * part : (t + 1) * part]
    beside = jnp.where(w > 0, 1, 0) + jnp.where(w < n_wire - 1, 1, 0)
    pl.semaphore_wait(barrier, n_energy - 1 + beside)

    def to_peer(src, dst, s_sem, r_sem, peer):
        return pltpu.make_async_remote_copy(
            src_ref=src.at[peer], dst_ref=dst.at[e], send_sem=s_sem.at[peer],
            recv_sem=r_sem.at[e], device_id={"energy": peer}, device_id_type=MESH)

    def from_peer(src, dst, s_sem, r_sem, peer):
        return pltpu.make_async_remote_copy(
            src_ref=src.at[peer], dst_ref=dst.at[peer], send_sem=s_sem.at[peer],
            recv_sem=r_sem.at[peer], device_id={"energy": peer}, device_id_type=MESH)

    def start_w(d, carry):
        to_peer(send_w, recv_w, sw_sem, rw_sem, lax.rem(e + d, n_energy)).start()
        return carry

    lax.fori_loop(1, n_energy, start_w, 0)
    recv_w[e] = send_w[e]

    for i in range(3):
        loads[i].wait()
    chunk = min(slots, 1024)

    def places(b, off, size):
        p = pat[b : b + 1, pl.ds(off, size)]
        slot = lax.broadcasted_iota(jnp.int32, (1, size), 1) + off
        row = jnp.where(slot < cnt_ref[b], lax.shift_right_logical(p, 7), n)
        col = lax.bitwise_and(p, 127)
        down = lax.broadcasted_iota(jnp.int32, (n, size), 0)
        return down == row, down == col

    acc[...] = jnp.zeros_like(acc)

    def scatter(i, carry):
        off = pl.multiple_of(i * chunk, chunk)
        for b in range(blocks):
            row_is, col_is = places(b, off, chunk)
            hot = jnp.where(row_is, 1.0, 0.0).astype(BF16)
            his, los = [], []
            for ref in (sl, sg):
                for p in range(2):
                    v = ref[p, b : b + 1, pl.ds(off, chunk)]
                    hi = v.astype(BF16).astype(F32)
                    his.append(jnp.where(col_is, hi, 0.0).astype(BF16))
                    los.append(jnp.where(col_is, v - hi, 0.0).astype(BF16))
            acc[b] += dot_nt(hot, jnp.concatenate(his + los, axis=0))
        return carry

    lax.fori_loop(0, slots // chunk, scatter, 0)

    loads[5].wait()
    loads[6].wait()
    mults = []
    total = None
    through = None
    for b in range(blocks):
        g_row = split(jnp.concatenate([g[0, b], g[1, b]], axis=1))
        c_row = split(jnp.concatenate([c[0, b], c[1, b]], axis=1))
        mult = split(dot3(dot_nn, g_row, full(c_row)))
        dense = acc[b]
        dense = dense[:, : 4 * n] + dense[:, 4 * n :]
        source = sandwich(g_row, full(g_row), jnp.stack([dense[:, : 2 * n], dense[:, 2 * n :]]))
        if b == 0:
            through = mult
            total = source
        else:
            square = full(mult)
            moved = sandwich(mult, square, st[b - 1])
            total = (source[0] + moved[0], source[1] + moved[1])
            through = split(dot3(dot_nn, mult, full(through)))
        st[b, 0] = total[0]
        st[b, 1] = total[1]
        mults.append(through)

    last = blocks - 1

    def ring(k):
        return pltpu.make_async_remote_copy(
            src_ref=st.at[last, k], dst_ref=pin.at[k], send_sem=ring_send.at[k],
            recv_sem=ring_recv.at[k], device_id={"wire": w + 1}, device_id_type=MESH)

    def arrive(k):
        return pltpu.make_async_remote_copy(
            src_ref=st.at[last, k], dst_ref=pin.at[k], send_sem=ring_send.at[k],
            recv_sem=ring_recv.at[k], device_id={"wire": w - 1}, device_id_type=MESH)

    def advance(b):
        more = sandwich(mults[b], full(mults[b]), pin[...])
        st[b, 0] += more[0]
        st[b, 1] += more[1]

    @pl.when(w > 0)
    def _():
        arrive(0).wait_recv()
        arrive(1).wait_recv()
        advance(last)

    @pl.when(w < n_wire - 1)
    def _():
        ring(0).start()
        ring(1).start()

    @pl.when(w > 0)
    def _():
        for b in range(last):
            advance(b)

    outs = []
    for b in range(blocks):
        for k, dst in enumerate((gl_hbm, gg_hbm)):
            for p in range(2):
                outs.append(pltpu.make_async_copy(
                    st.at[b, k, :, pl.ds(p * n, n)], dst.at[p, b], out_sem.at[len(outs)]))
    for copy in outs:
        copy.start()

    for b in range(blocks):
        for k in range(2):
            hi, lo = split(st[b, k])
            for p in range(2):
                at = (2 * k + p) * n
                lhs[b, at : at + n, :n] = hi[:, p * n : (p + 1) * n]
                lhs[b, at : at + n, n:] = lo[:, p * n : (p + 1) * n]

    def gather(d, carry):
        t = lax.rem(e + d, n_energy)
        off = pl.multiple_of(t * part, part)
        for b in range(blocks):
            row_is, col_is = places(b, off, part)
            hot = jnp.where(col_is, 1.0, 0.0).astype(BF16)
            taken = dot_nn(lhs[b], jnp.concatenate([hot, hot], axis=0))
            for k in range(2):
                for p in range(2):
                    at = (2 * k + p) * n
                    row = p * 2 * blocks + k * blocks + b
                    picked = jnp.where(row_is, taken[at : at + n], 0.0)
                    send_g[t, row : row + 1, :] = jnp.sum(picked, axis=0, keepdims=True)

        @pl.when(d < n_energy)
        def _():
            to_peer(send_g, recv_g, sg_sem, rg_sem, t).start()

        return carry

    lax.fori_loop(1, n_energy + 1, gather, 0)
    recv_g[e] = send_g[e]

    def land(d, carry):
        peer = lax.rem(e + d, n_energy)
        from_peer(send_w, recv_w, sw_sem, rw_sem, peer).wait_recv()
        from_peer(send_g, recv_g, sg_sem, rg_sem, peer).wait_recv()
        return carry

    lax.fori_loop(1, n_energy, land, 0)

    half = rows // 2
    scale = n_energy ** -0.5
    plain, turned, straight, crossed = [], [], [], []
    for k in range(n_energy):
        x = recv_g[k]
        y = recv_w[k]
        plain.append(x)
        turned.append(jnp.concatenate([x[half:], x[:half]], axis=0))
        straight.append(jnp.concatenate([y[:half], y[:half]], axis=0))
        crossed.append(jnp.concatenate([-y[half:], y[half:]], axis=0))
    for f in range(n_energy):
        total = None
        for k in range(f + 1):
            term = plain[f - k] * straight[k] + turned[f - k] * crossed[k]
            total = term if total is None else total + term
        send_s[f] = jnp.concatenate([-scale * total[half:], scale * total[:half]], axis=0)

        @pl.when(e != f)
        def _():
            to_peer(send_s, recv_s, ss_sem, rs_sem, f).start()

    recv_s[e] = send_s[e]

    def land_s(d, carry):
        peer = lax.rem(e + d, n_energy)
        from_peer(send_s, recv_s, ss_sem, rs_sem, peer).wait_recv()
        return carry

    lax.fori_loop(1, n_energy, land_s, 0)
    for t in range(n_energy):
        for p in range(2):
            for k, ref in enumerate((ol_ref, og_ref)):
                for b in range(blocks):
                    row = p * 2 * blocks + k * blocks + b
                    ref[p, b : b + 1, t * part : (t + 1) * part] = recv_s[t, row : row + 1, :]

    def drain(d, carry):
        peer = lax.rem(e + d, n_energy)
        to_peer(send_w, recv_w, sw_sem, rw_sem, peer).wait_send()
        to_peer(send_g, recv_g, sg_sem, rg_sem, peer).wait_send()
        to_peer(send_s, recv_s, ss_sem, rs_sem, peer).wait_send()
        return carry

    lax.fori_loop(1, n_energy, drain, 0)

    @pl.when(w < n_wire - 1)
    def _():
        ring(0).wait_send()
        ring(1).wait_send()

    for copy in outs:
        copy.wait()


def on_device(n_energy, n_wire, green_ret, coupling, sl, sg, wl, wg, pattern, counts):
    blocks, n = green_ret.shape[2], green_ret.shape[3]
    slots = pattern.shape[1]
    part = slots // n_energy
    rows = 4 * blocks
    g = green_ret.reshape(2, blocks, n, n)
    vals = [x.reshape(2, blocks, slots) for x in (sl, sg, wl, wg)]
    any_spec = pl.BlockSpec(memory_space=pl.ANY)
    hbm_spec = pl.BlockSpec(memory_space=pltpu.HBM)
    vmem_spec = pl.BlockSpec(memory_space=pltpu.VMEM)
    dma = pltpu.SemaphoreType.DMA
    mail = pltpu.VMEM((n_energy, rows, part), F32)
    out = pl.pallas_call(
        functools.partial(kernel, n_energy, n_wire),
        out_shape=[
            jax.ShapeDtypeStruct((2, blocks, n, n), F32),
            jax.ShapeDtypeStruct((2, blocks, n, n), F32),
            jax.ShapeDtypeStruct((2, blocks, slots), F32),
            jax.ShapeDtypeStruct((2, blocks, slots), F32),
        ],
        in_specs=[hbm_spec] * 7 + [pl.BlockSpec(memory_space=pltpu.SMEM)],
        out_specs=[any_spec, any_spec, vmem_spec, vmem_spec],
        scratch_shapes=[
            pltpu.VMEM((2, blocks, n, n), F32),
            pltpu.VMEM((2, blocks, n, n), F32),
            pltpu.VMEM((2, blocks, slots), F32),
            pltpu.VMEM((2, blocks, slots), F32),
            pltpu.VMEM((2, blocks, slots), F32),
            pltpu.VMEM((2, blocks, slots), F32),
            pltpu.VMEM((blocks, slots), jnp.int32),
            pltpu.VMEM((blocks, n, 8 * n), F32),
            pltpu.VMEM((blocks, 2, n, 2 * n), F32),
            pltpu.VMEM((2, n, 2 * n), F32),
            pltpu.VMEM((blocks, 4 * n, 2 * n), BF16),
            mail, mail, mail, mail, mail, mail,
            dma((7,)), dma((4 * blocks,)), dma((2,)), dma((2,)),
            dma((n_energy,)), dma((n_energy,)), dma((n_energy,)),
            dma((n_energy,)), dma((n_energy,)), dma((n_energy,)),
        ],
        compiler_params=pltpu.CompilerParams(
            collective_id=0, has_side_effects=True, vmem_limit_bytes=40 * 1024 * 1024
        ),
    )(g, coupling, *vals, pattern, counts)
    return (
        out[0].reshape(green_ret.shape),
        out[1].reshape(green_ret.shape),
        out[2].reshape(sl.shape),
        out[3].reshape(sl.shape),
    )


def solution(mesh):
    blocks_spec = P(None, "energy", "wire", None, None)
    slots_spec = P(None, "energy", "wire", None)
    in_specs = (
        blocks_spec, P(None, "wire", None, None),
        slots_spec, slots_spec, slots_spec, slots_spec,
        P("wire", None), P("wire"),
    )
    out_specs = (blocks_spec, blocks_spec, slots_spec, slots_spec)
    return jax.shard_map(
        functools.partial(on_device, mesh.shape["energy"], mesh.shape["wire"]),
        mesh=mesh, in_specs=in_specs, out_specs=out_specs, check_vma=False,
    )
```

```python
import functools

import jax
import jax.numpy as jnp
from jax import lax
from jax.experimental import pallas as pl
from jax.experimental.pallas import tpu as pltpu
from jax.sharding import PartitionSpec as P

MESH = pl.DeviceIdType.MESH
F32 = jnp.float32
BF16 = jnp.bfloat16


def split(x):
    hi = x.astype(BF16)
    lo = (x - hi.astype(F32)).astype(BF16)
    return hi, lo


def dot_nn(a, b):
    return lax.dot_general(a, b, (((1,), (0,)), ((), ())), preferred_element_type=F32)


def dot_nt(a, b):
    return lax.dot_general(a, b, (((1,), (1,)), ((), ())), preferred_element_type=F32)


def dot3(dot, a, b):
    return dot(a[0], b[0]) + (dot(a[1], b[0]) + dot(a[0], b[1]))


def full_one(row):
    n = row.shape[1] // 2
    re, im = row[:, :n], row[:, n:]
    return jnp.concatenate(
        [jnp.concatenate([re, im], axis=1), jnp.concatenate([-im, re], axis=1)], axis=0
    )


def full(row):
    return full_one(row[0]), full_one(row[1])


def sandwich(row, square, state):
    n = row[0].shape[0]
    stacked = state.reshape(2 * n, 2 * n)
    right = dot3(dot_nt, split(stacked), square)
    hi, lo = split(right)
    wide = tuple(
        jnp.concatenate([full_one(x[:n]), full_one(x[n:])], axis=1) for x in (hi, lo)
    )
    out = dot3(dot_nn, row, wide)
    return out[:, : 2 * n], out[:, 2 * n :]


def kernel(
    n_energy, n_wire,
    g_hbm, c_hbm, sl_hbm, sg_hbm, wl_hbm, wg_hbm, pat_hbm, cnt_ref,
    gl_hbm, gg_hbm, ol_ref, og_ref,
    g, c, sl, sg, wl, wg, pat,
    acc, st, pin, lhs, send_w, recv_w, send_g, recv_g, send_s, recv_s,
    in_sem, out_sem, ring_send, ring_recv, sw_sem, rw_sem, sg_sem, rg_sem, ss_sem, rs_sem,
):
    e = lax.axis_index("energy")
    w = lax.axis_index("wire")
    blocks = g.shape[1]
    n = g.shape[2]
    slots = pat.shape[1]
    part = slots // n_energy
    rows = 4 * blocks

    barrier = pltpu.get_barrier_semaphore()

    def greet(d, carry):
        peer = lax.rem(e + d, n_energy)
        pl.semaphore_signal(barrier, inc=1, device_id={"energy": peer}, device_id_type=MESH)
        return carry

    lax.fori_loop(1, n_energy, greet, 0)

    @pl.when(w > 0)
    def _():
        pl.semaphore_signal(barrier, inc=1, device_id={"wire": w - 1}, device_id_type=MESH)

    @pl.when(w < n_wire - 1)
    def _():
        pl.semaphore_signal(barrier, inc=1, device_id={"wire": w + 1}, device_id_type=MESH)

    pairs = [(pat_hbm, pat), (sl_hbm, sl), (sg_hbm, sg), (wl_hbm, wl), (wg_hbm, wg),
             (g_hbm, g), (c_hbm, c)]
    loads = [pltpu.make_async_copy(s, d, in_sem.at[i]) for i, (s, d) in enumerate(pairs)]
    for copy in loads:
        copy.start()

    loads[3].wait()
    loads[4].wait()
    for t in range(n_energy):
        for p in range(2):
            for k, ref in enumerate((wl, wg)):
                for b in range(blocks):
                    row = p * 2 * blocks + k * blocks + b
                    send_w[t, row : row + 1, :] = ref[p, b : b + 1, t * part : (t + 1) * part]
    beside = jnp.where(w > 0, 1, 0) + jnp.where(w < n_wire - 1, 1, 0)
    pl.semaphore_wait(barrier, n_energy - 1 + beside)

    def to_peer(src, dst, s_sem, r_sem, peer):
        return pltpu.make_async_remote_copy(
            src_ref=src.at[peer], dst_ref=dst.at[e], send_sem=s_sem.at[peer],
            recv_sem=r_sem.at[e], device_id={"energy": peer}, device_id_type=MESH)

    def from_peer(src, dst, s_sem, r_sem, peer):
        return pltpu.make_async_remote_copy(
            src_ref=src.at[peer], dst_ref=dst.at[peer], send_sem=s_sem.at[peer],
            recv_sem=r_sem.at[peer], device_id={"energy": peer}, device_id_type=MESH)

    def start_w(d, carry):
        to_peer(send_w, recv_w, sw_sem, rw_sem, lax.rem(e + d, n_energy)).start()
        return carry

    lax.fori_loop(1, n_energy, start_w, 0)
    recv_w[e] = send_w[e]

    for i in range(3):
        loads[i].wait()
    chunk = min(slots, 1024)

    def places(b, off, size):
        p = pat[b : b + 1, pl.ds(off, size)]
        slot = lax.broadcasted_iota(jnp.int32, (1, size), 1) + off
        row = jnp.where(slot < cnt_ref[b], lax.shift_right_logical(p, 7), n)
        col = lax.bitwise_and(p, 127)
        down = lax.broadcasted_iota(jnp.int32, (n, size), 0)
        return down == row, down == col

    acc[...] = jnp.zeros_like(acc)

    def scatter(i, carry):
        off = pl.multiple_of(i * chunk, chunk)
        for b in range(blocks):
            row_is, col_is = places(b, off, chunk)
            hot = jnp.where(row_is, 1.0, 0.0).astype(BF16)
            his, los = [], []
            for ref in (sl, sg):
                for p in range(2):
                    v = ref[p, b : b + 1, pl.ds(off, chunk)]
                    hi = v.astype(BF16).astype(F32)
                    his.append(jnp.where(col_is, hi, 0.0).astype(BF16))
                    los.append(jnp.where(col_is, v - hi, 0.0).astype(BF16))
            acc[b] += dot_nt(hot, jnp.concatenate(his + los, axis=0))
        return carry

    lax.fori_loop(0, slots // chunk, scatter, 0)

    loads[5].wait()
    loads[6].wait()
    mults = []
    total = None
    through = None
    for b in range(blocks):
        g_row = split(jnp.concatenate([g[0, b], g[1, b]], axis=1))
        c_row = split(jnp.concatenate([c[0, b], c[1, b]], axis=1))
        mult = split(dot3(dot_nn, g_row, full(c_row)))
        dense = acc[b]
        dense = dense[:, : 4 * n] + dense[:, 4 * n :]
        source = sandwich(g_row, full(g_row), jnp.stack([dense[:, : 2 * n], dense[:, 2 * n :]]))
        if b == 0:
            through = mult
            total = source
        else:
            square = full(mult)
            moved = sandwich(mult, square, st[b - 1])
            total = (source[0] + moved[0], source[1] + moved[1])
            through = split(dot3(dot_nn, mult, full(through)))
        st[b, 0] = total[0]
        st[b, 1] = total[1]
        mults.append(through)

    last = blocks - 1

    def ring(k):
        return pltpu.make_async_remote_copy(
            src_ref=st.at[last, k], dst_ref=pin.at[k], send_sem=ring_send.at[k],
            recv_sem=ring_recv.at[k], device_id={"wire": w + 1}, device_id_type=MESH)

    def arrive(k):
        return pltpu.make_async_remote_copy(
            src_ref=st.at[last, k], dst_ref=pin.at[k], send_sem=ring_send.at[k],
            recv_sem=ring_recv.at[k], device_id={"wire": w - 1}, device_id_type=MESH)

    def advance(b):
        more = sandwich(mults[b], full(mults[b]), pin[...])
        st[b, 0] += more[0]
        st[b, 1] += more[1]

    @pl.when(w > 0)
    def _():
        arrive(0).wait_recv()
        arrive(1).wait_recv()
        advance(last)

    @pl.when(w < n_wire - 1)
    def _():
        ring(0).start()
        ring(1).start()

    @pl.when(w > 0)
    def _():
        for b in range(last):
            advance(b)

    outs = []
    for b in range(blocks):
        for k, dst in enumerate((gl_hbm, gg_hbm)):
            for p in range(2):
                outs.append(pltpu.make_async_copy(
                    st.at[b, k, :, pl.ds(p * n, n)], dst.at[p, b], out_sem.at[len(outs)]))
    for copy in outs:
        copy.start()

    for b in range(blocks):
        for k in range(2):
            hi, lo = split(st[b, k])
            for p in range(2):
                at = (2 * k + p) * n
                lhs[b, at : at + n, :n] = hi[:, p * n : (p + 1) * n]
                lhs[b, at : at + n, n:] = lo[:, p * n : (p + 1) * n]

    def gather(d, carry):
        t = lax.rem(e + d, n_energy)
        off = pl.multiple_of(t * part, part)
        for b in range(blocks):
            row_is, col_is = places(b, off, part)
            hot = jnp.where(col_is, 1.0, 0.0).astype(BF16)
            taken = dot_nn(lhs[b], jnp.concatenate([hot, hot], axis=0))
            for k in range(2):
                for p in range(2):
                    at = (2 * k + p) * n
                    row = p * 2 * blocks + k * blocks + b
                    picked = jnp.where(row_is, taken[at : at + n], 0.0)
                    send_g[t, row : row + 1, :] = jnp.sum(picked, axis=0, keepdims=True)

        @pl.when(d < n_energy)
        def _():
            to_peer(send_g, recv_g, sg_sem, rg_sem, t).start()

        return carry

    lax.fori_loop(1, n_energy + 1, gather, 0)
    recv_g[e] = send_g[e]

    def land(d, carry):
        peer = lax.rem(e + d, n_energy)
        from_peer(send_w, recv_w, sw_sem, rw_sem, peer).wait_recv()
        from_peer(send_g, recv_g, sg_sem, rg_sem, peer).wait_recv()
        return carry

    lax.fori_loop(1, n_energy, land, 0)

    half = rows // 2
    scale = n_energy ** -0.5
    plain, turned, straight, crossed = [], [], [], []
    for k in range(n_energy):
        x = recv_g[k]
        y = recv_w[k]
        plain.append(x)
        turned.append(jnp.concatenate([x[half:], x[:half]], axis=0))
        straight.append(jnp.concatenate([y[:half], y[:half]], axis=0))
        crossed.append(jnp.concatenate([-y[half:], y[half:]], axis=0))
    for f in range(n_energy):
        total = None
        for k in range(f + 1):
            term = plain[f - k] * straight[k] + turned[f - k] * crossed[k]
            total = term if total is None else total + term
        send_s[f] = jnp.concatenate([-scale * total[half:], scale * total[:half]], axis=0)

        @pl.when(e != f)
        def _():
            to_peer(send_s, recv_s, ss_sem, rs_sem, f).start()

    recv_s[e] = send_s[e]

    def land_s(d, carry):
        peer = lax.rem(e + d, n_energy)
        from_peer(send_s, recv_s, ss_sem, rs_sem, peer).wait_recv()
        return carry

    lax.fori_loop(1, n_energy, land_s, 0)
    for t in range(n_energy):
        for p in range(2):
            for k, ref in enumerate((ol_ref, og_ref)):
                for b in range(blocks):
                    row = p * 2 * blocks + k * blocks + b
                    ref[p, b : b + 1, t * part : (t + 1) * part] = recv_s[t, row : row + 1, :]

    def drain(d, carry):
        peer = lax.rem(e + d, n_energy)
        to_peer(send_w, recv_w, sw_sem, rw_sem, peer).wait_send()
        to_peer(send_g, recv_g, sg_sem, rg_sem, peer).wait_send()
        to_peer(send_s, recv_s, ss_sem, rs_sem, peer).wait_send()
        return carry

    lax.fori_loop(1, n_energy, drain, 0)

    @pl.when(w < n_wire - 1)
    def _():
        ring(0).wait_send()
        ring(1).wait_send()

    for copy in outs:
        copy.wait()


def hand_over(*refs):
    count = (len(refs) - 1) // 2
    copies = [
        pltpu.make_async_copy(refs[i], refs[count + i], refs[-1].at[i]) for i in range(count)
    ]
    for copy in copies:
        copy.start()
    for copy in copies:
        copy.wait()


def on_device(n_energy, n_wire, green_ret, coupling, sl, sg, wl, wg, pattern, counts):
    blocks, n = green_ret.shape[2], green_ret.shape[3]
    slots = pattern.shape[1]
    part = slots // n_energy
    rows = 4 * blocks
    g = green_ret.reshape(2, blocks, n, n)
    vals = [x.reshape(2, blocks, slots) for x in (sl, sg, wl, wg)]
    any_spec = pl.BlockSpec(memory_space=pl.ANY)
    hbm_spec = pl.BlockSpec(memory_space=pltpu.HBM)
    vmem_spec = pl.BlockSpec(memory_space=pltpu.VMEM)
    dma = pltpu.SemaphoreType.DMA
    mail = pltpu.VMEM((n_energy, rows, part), F32)
    out = pl.pallas_call(
        functools.partial(kernel, n_energy, n_wire),
        out_shape=[
            jax.ShapeDtypeStruct((2, blocks, n, n), F32),
            jax.ShapeDtypeStruct((2, blocks, n, n), F32),
            jax.ShapeDtypeStruct((2, blocks, slots), F32),
            jax.ShapeDtypeStruct((2, blocks, slots), F32),
        ],
        in_specs=[hbm_spec] * 7 + [pl.BlockSpec(memory_space=pltpu.SMEM)],
        out_specs=[any_spec, any_spec, vmem_spec, vmem_spec],
        scratch_shapes=[
            pltpu.VMEM((2, blocks, n, n), F32),
            pltpu.VMEM((2, blocks, n, n), F32),
            pltpu.VMEM((2, blocks, slots), F32),
            pltpu.VMEM((2, blocks, slots), F32),
            pltpu.VMEM((2, blocks, slots), F32),
            pltpu.VMEM((2, blocks, slots), F32),
            pltpu.VMEM((blocks, slots), jnp.int32),
            pltpu.VMEM((blocks, n, 8 * n), F32),
            pltpu.VMEM((blocks, 2, n, 2 * n), F32),
            pltpu.VMEM((2, n, 2 * n), F32),
            pltpu.VMEM((blocks, 4 * n, 2 * n), BF16),
            mail, mail, mail, mail, mail, mail,
            dma((7,)), dma((4 * blocks,)), dma((2,)), dma((2,)),
            dma((n_energy,)), dma((n_energy,)), dma((n_energy,)),
            dma((n_energy,)), dma((n_energy,)), dma((n_energy,)),
        ],
        compiler_params=pltpu.CompilerParams(
            collective_id=0, has_side_effects=True, vmem_limit_bytes=60 * 1024 * 1024
        ),
    )(g, coupling, *vals, pattern, counts)
    out = pl.pallas_call(
        hand_over,
        out_shape=[jax.ShapeDtypeStruct(x.shape, x.dtype) for x in out],
        in_specs=[hbm_spec] * 4,
        out_specs=[hbm_spec] * 4,
        scratch_shapes=[dma((4,))],
        compiler_params=pltpu.CompilerParams(vmem_limit_bytes=60 * 1024 * 1024),
    )(*out)
    return (
        out[0].reshape(green_ret.shape),
        out[1].reshape(green_ret.shape),
        out[2].reshape(sl.shape),
        out[3].reshape(sl.shape),
    )


def solution(mesh):
    blocks_spec = P(None, "energy", "wire", None, None)
    slots_spec = P(None, "energy", "wire", None)
    in_specs = (
        blocks_spec, P(None, "wire", None, None),
        slots_spec, slots_spec, slots_spec, slots_spec,
        P("wire", None), P("wire"),
    )
    out_specs = (blocks_spec, blocks_spec, slots_spec, slots_spec)
    return jax.shard_map(
        functools.partial(on_device, mesh.shape["energy"], mesh.shape["wire"]),
        mesh=mesh, in_specs=in_specs, out_specs=out_specs, check_vma=False,
    )
```

```python
import functools

import jax
import jax.numpy as jnp
from jax import lax
from jax.experimental import pallas as pl
from jax.experimental.pallas import tpu as pltpu
from jax.sharding import PartitionSpec as P

MESH = pl.DeviceIdType.MESH
F32 = jnp.float32
BF16 = jnp.bfloat16


def split(x):
    hi = x.astype(BF16)
    lo = (x - hi.astype(F32)).astype(BF16)
    return hi, lo


def dot_nn(a, b):
    return lax.dot_general(a, b, (((1,), (0,)), ((), ())), preferred_element_type=F32)


def dot_nt(a, b):
    return lax.dot_general(a, b, (((1,), (1,)), ((), ())), preferred_element_type=F32)


def dot3(dot, a, b):
    return dot(a[0], b[0]) + (dot(a[1], b[0]) + dot(a[0], b[1]))


def full_one(row):
    n = row.shape[1] // 2
    re, im = row[:, :n], row[:, n:]
    return jnp.concatenate(
        [jnp.concatenate([re, im], axis=1), jnp.concatenate([-im, re], axis=1)], axis=0
    )


def full(row):
    return full_one(row[0]), full_one(row[1])


def sandwich(row, square, state):
    n = row[0].shape[0]
    stacked = state.reshape(2 * n, 2 * n)
    right = dot3(dot_nt, split(stacked), square)
    hi, lo = split(right)
    wide = tuple(
        jnp.concatenate([full_one(x[:n]), full_one(x[n:])], axis=1) for x in (hi, lo)
    )
    out = dot3(dot_nn, row, wide)
    return out[:, : 2 * n], out[:, 2 * n :]


def kernel(
    n_energy, n_wire,
    g_hbm, c_hbm, sl_hbm, sg_hbm, wl_hbm, wg_hbm, pat_hbm, cnt_hbm,
    st, ol_ref, og_ref,
    g, c, sl, sg, wl, wg, pat, cnt_ref,
    acc, pin, lhs, send_w, recv_w, send_g, recv_g, send_s, recv_s,
    in_sem, ring_send, ring_recv, sw_sem, rw_sem, sg_sem, rg_sem, ss_sem, rs_sem,
):
    e = lax.axis_index("energy")
    w = lax.axis_index("wire")
    blocks = g.shape[1]
    n = g.shape[2]
    slots = pat.shape[1]
    part = slots // n_energy
    rows = 4 * blocks

    barrier = pltpu.get_barrier_semaphore()

    def greet(d, carry):
        peer = lax.rem(e + d, n_energy)
        pl.semaphore_signal(barrier, inc=1, device_id={"energy": peer}, device_id_type=MESH)
        return carry

    lax.fori_loop(1, n_energy, greet, 0)

    @pl.when(w > 0)
    def _():
        pl.semaphore_signal(barrier, inc=1, device_id={"wire": w - 1}, device_id_type=MESH)

    @pl.when(w < n_wire - 1)
    def _():
        pl.semaphore_signal(barrier, inc=1, device_id={"wire": w + 1}, device_id_type=MESH)

    pairs = [(pat_hbm, pat), (sl_hbm, sl), (sg_hbm, sg), (wl_hbm, wl), (wg_hbm, wg),
             (g_hbm, g), (c_hbm, c), (cnt_hbm, cnt_ref)]
    loads = [pltpu.make_async_copy(s, d, in_sem.at[i]) for i, (s, d) in enumerate(pairs)]
    for copy in loads:
        copy.start()

    loads[3].wait()
    loads[4].wait()
    for t in range(n_energy):
        for p in range(2):
            for k, ref in enumerate((wl, wg)):
                for b in range(blocks):
                    row = p * 2 * blocks + k * blocks + b
                    send_w[t, row : row + 1, :] = ref[p, b : b + 1, t * part : (t + 1) * part]
    beside = jnp.where(w > 0, 1, 0) + jnp.where(w < n_wire - 1, 1, 0)
    pl.semaphore_wait(barrier, n_energy - 1 + beside)

    def to_peer(src, dst, s_sem, r_sem, peer):
        return pltpu.make_async_remote_copy(
            src_ref=src.at[peer], dst_ref=dst.at[e], send_sem=s_sem.at[peer],
            recv_sem=r_sem.at[e], device_id={"energy": peer}, device_id_type=MESH)

    def from_peer(src, dst, s_sem, r_sem, peer):
        return pltpu.make_async_remote_copy(
            src_ref=src.at[peer], dst_ref=dst.at[peer], send_sem=s_sem.at[peer],
            recv_sem=r_sem.at[peer], device_id={"energy": peer}, device_id_type=MESH)

    def start_w(d, carry):
        to_peer(send_w, recv_w, sw_sem, rw_sem, lax.rem(e + d, n_energy)).start()
        return carry

    lax.fori_loop(1, n_energy, start_w, 0)
    recv_w[e] = send_w[e]

    for i in (0, 1, 2, 7):
        loads[i].wait()
    chunk = min(slots, 1024)

    def places(b, off, size):
        p = pat[b : b + 1, pl.ds(off, size)]
        slot = lax.broadcasted_iota(jnp.int32, (1, size), 1) + off
        row = jnp.where(slot < cnt_ref[b], lax.shift_right_logical(p, 7), n)
        col = lax.bitwise_and(p, 127)
        down = lax.broadcasted_iota(jnp.int32, (n, size), 0)
        return down == row, down == col

    acc[...] = jnp.zeros_like(acc)

    def scatter(i, carry):
        off = pl.multiple_of(i * chunk, chunk)
        for b in range(blocks):
            row_is, col_is = places(b, off, chunk)
            hot = jnp.where(row_is, 1.0, 0.0).astype(BF16)
            his, los = [], []
            for ref in (sl, sg):
                for p in range(2):
                    v = ref[p, b : b + 1, pl.ds(off, chunk)]
                    hi = v.astype(BF16).astype(F32)
                    his.append(jnp.where(col_is, hi, 0.0).astype(BF16))
                    los.append(jnp.where(col_is, v - hi, 0.0).astype(BF16))
            acc[b] += dot_nt(hot, jnp.concatenate(his + los, axis=0))
        return carry

    lax.fori_loop(0, slots // chunk, scatter, 0)

    loads[5].wait()
    loads[6].wait()
    mults = []
    total = None
    through = None
    for b in range(blocks):
        g_row = split(jnp.concatenate([g[0, b], g[1, b]], axis=1))
        c_row = split(jnp.concatenate([c[0, b], c[1, b]], axis=1))
        mult = split(dot3(dot_nn, g_row, full(c_row)))
        dense = acc[b]
        dense = dense[:, : 4 * n] + dense[:, 4 * n :]
        source = sandwich(g_row, full(g_row), jnp.stack([dense[:, : 2 * n], dense[:, 2 * n :]]))
        if b == 0:
            through = mult
            total = source
        else:
            square = full(mult)
            moved = sandwich(mult, square, st[b - 1])
            total = (source[0] + moved[0], source[1] + moved[1])
            through = split(dot3(dot_nn, mult, full(through)))
        st[b, 0] = total[0]
        st[b, 1] = total[1]
        mults.append(through)

    last = blocks - 1

    def ring(k):
        return pltpu.make_async_remote_copy(
            src_ref=st.at[last, k], dst_ref=pin.at[k], send_sem=ring_send.at[k],
            recv_sem=ring_recv.at[k], device_id={"wire": w + 1}, device_id_type=MESH)

    def arrive(k):
        return pltpu.make_async_remote_copy(
            src_ref=st.at[last, k], dst_ref=pin.at[k], send_sem=ring_send.at[k],
            recv_sem=ring_recv.at[k], device_id={"wire": w - 1}, device_id_type=MESH)

    def advance(b):
        more = sandwich(mults[b], full(mults[b]), pin[...])
        st[b, 0] += more[0]
        st[b, 1] += more[1]

    @pl.when(w > 0)
    def _():
        arrive(0).wait_recv()
        arrive(1).wait_recv()
        advance(last)

    @pl.when(w < n_wire - 1)
    def _():
        ring(0).start()
        ring(1).start()

    @pl.when(w > 0)
    def _():
        for b in range(last):
            advance(b)

    for b in range(blocks):
        for k in range(2):
            hi, lo = split(st[b, k])
            for p in range(2):
                at = (2 * k + p) * n
                lhs[b, at : at + n, :n] = hi[:, p * n : (p + 1) * n]
                lhs[b, at : at + n, n:] = lo[:, p * n : (p + 1) * n]

    def gather(d, carry):
        t = lax.rem(e + d, n_energy)
        off = pl.multiple_of(t * part, part)
        for b in range(blocks):
            row_is, col_is = places(b, off, part)
            hot = jnp.where(col_is, 1.0, 0.0).astype(BF16)
            taken = dot_nn(lhs[b], jnp.concatenate([hot, hot], axis=0))
            for k in range(2):
                for p in range(2):
                    at = (2 * k + p) * n
                    row = p * 2 * blocks + k * blocks + b
                    picked = jnp.where(row_is, taken[at : at + n], 0.0)
                    send_g[t, row : row + 1, :] = jnp.sum(picked, axis=0, keepdims=True)

        @pl.when(d < n_energy)
        def _():
            to_peer(send_g, recv_g, sg_sem, rg_sem, t).start()

        return carry

    lax.fori_loop(1, n_energy + 1, gather, 0)
    recv_g[e] = send_g[e]

    def land(d, carry):
        peer = lax.rem(e + d, n_energy)
        from_peer(send_w, recv_w, sw_sem, rw_sem, peer).wait_recv()
        from_peer(send_g, recv_g, sg_sem, rg_sem, peer).wait_recv()
        return carry

    lax.fori_loop(1, n_energy, land, 0)

    half = rows // 2
    scale = n_energy ** -0.5
    plain, turned, straight, crossed = [], [], [], []
    for k in range(n_energy):
        x = recv_g[k]
        y = recv_w[k]
        plain.append(x)
        turned.append(jnp.concatenate([x[half:], x[:half]], axis=0))
        straight.append(jnp.concatenate([y[:half], y[:half]], axis=0))
        crossed.append(jnp.concatenate([-y[half:], y[half:]], axis=0))
    for f in range(n_energy):
        total = None
        for k in range(f + 1):
            term = plain[f - k] * straight[k] + turned[f - k] * crossed[k]
            total = term if total is None else total + term
        send_s[f] = jnp.concatenate([-scale * total[half:], scale * total[:half]], axis=0)

        @pl.when(e != f)
        def _():
            to_peer(send_s, recv_s, ss_sem, rs_sem, f).start()

    recv_s[e] = send_s[e]

    def land_s(d, carry):
        peer = lax.rem(e + d, n_energy)
        from_peer(send_s, recv_s, ss_sem, rs_sem, peer).wait_recv()
        return carry

    lax.fori_loop(1, n_energy, land_s, 0)
    for t in range(n_energy):
        for p in range(2):
            for k, ref in enumerate((ol_ref, og_ref)):
                for b in range(blocks):
                    row = p * 2 * blocks + k * blocks + b
                    ref[p, b : b + 1, t * part : (t + 1) * part] = recv_s[t, row : row + 1, :]

    def drain(d, carry):
        peer = lax.rem(e + d, n_energy)
        to_peer(send_w, recv_w, sw_sem, rw_sem, peer).wait_send()
        to_peer(send_g, recv_g, sg_sem, rg_sem, peer).wait_send()
        to_peer(send_s, recv_s, ss_sem, rs_sem, peer).wait_send()
        return carry

    lax.fori_loop(1, n_energy, drain, 0)

    @pl.when(w < n_wire - 1)
    def _():
        ring(0).wait_send()
        ring(1).wait_send()


def hand_over(st, ol, og, gl_hbm, gg_hbm, ol_hbm, og_hbm, sem):
    blocks, n = st.shape[0], st.shape[2]
    pairs = [(ol, ol_hbm), (og, og_hbm)]
    for b in range(blocks):
        for k, dst in enumerate((gl_hbm, gg_hbm)):
            for p in range(2):
                pairs.append((st.at[b, k, :, pl.ds(p * n, n)], dst.at[p, b]))
    copies = [pltpu.make_async_copy(s, d, sem.at[i]) for i, (s, d) in enumerate(pairs)]
    for copy in copies:
        copy.start()
    for copy in copies:
        copy.wait()


def on_device(n_energy, n_wire, green_ret, coupling, sl, sg, wl, wg, pattern, counts):
    blocks, n = green_ret.shape[2], green_ret.shape[3]
    slots = pattern.shape[1]
    part = slots // n_energy
    rows = 4 * blocks
    g = green_ret.reshape(2, blocks, n, n)
    vals = [x.reshape(2, blocks, slots) for x in (sl, sg, wl, wg)]
    hbm_spec = pl.BlockSpec(memory_space=pltpu.HBM)
    vmem_spec = pl.BlockSpec(memory_space=pltpu.VMEM)
    dma = pltpu.SemaphoreType.DMA
    mail = pltpu.VMEM((n_energy, rows, part), F32)
    out = pl.pallas_call(
        functools.partial(kernel, n_energy, n_wire),
        out_shape=[
            pltpu.VMEM((blocks, 2, n, 2 * n), F32),
            pltpu.VMEM((2, blocks, slots), F32),
            pltpu.VMEM((2, blocks, slots), F32),
        ],
        in_specs=[hbm_spec] * 8,
        out_specs=[vmem_spec] * 3,
        scratch_shapes=[
            pltpu.VMEM((2, blocks, n, n), F32),
            pltpu.VMEM((2, blocks, n, n), F32),
            pltpu.VMEM((2, blocks, slots), F32),
            pltpu.VMEM((2, blocks, slots), F32),
            pltpu.VMEM((2, blocks, slots), F32),
            pltpu.VMEM((2, blocks, slots), F32),
            pltpu.VMEM((blocks, slots), jnp.int32),
            pltpu.SMEM((blocks,), jnp.int32),
            pltpu.VMEM((blocks, n, 8 * n), F32),
            pltpu.VMEM((2, n, 2 * n), F32),
            pltpu.VMEM((blocks, 4 * n, 2 * n), BF16),
            mail, mail, mail, mail, mail, mail,
            dma((8,)), dma((2,)), dma((2,)),
            dma((n_energy,)), dma((n_energy,)), dma((n_energy,)),
            dma((n_energy,)), dma((n_energy,)), dma((n_energy,)),
        ],
        compiler_params=pltpu.CompilerParams(
            collective_id=0, has_side_effects=True, vmem_limit_bytes=40 * 1024 * 1024
        ),
    )(*[pltpu.with_memory_space_constraint(x, pltpu.HBM) for x in (g, coupling, *vals, pattern, counts)])
    out = pl.pallas_call(
        hand_over,
        out_shape=[
            jax.ShapeDtypeStruct((2, blocks, n, n), F32),
            jax.ShapeDtypeStruct((2, blocks, n, n), F32),
            jax.ShapeDtypeStruct((2, blocks, slots), F32),
            jax.ShapeDtypeStruct((2, blocks, slots), F32),
        ],
        in_specs=[vmem_spec] * 3,
        out_specs=[hbm_spec] * 4,
        scratch_shapes=[dma((2 + 4 * blocks,))],
    )(*[pltpu.with_memory_space_constraint(x, pltpu.VMEM) for x in out])
    return (
        out[0].reshape(green_ret.shape),
        out[1].reshape(green_ret.shape),
        out[2].reshape(sl.shape),
        out[3].reshape(sl.shape),
    )


def solution(mesh):
    blocks_spec = P(None, "energy", "wire", None, None)
    slots_spec = P(None, "energy", "wire", None)
    in_specs = (
        blocks_spec, P(None, "wire", None, None),
        slots_spec, slots_spec, slots_spec, slots_spec,
        P("wire", None), P("wire"),
    )
    out_specs = (blocks_spec, blocks_spec, slots_spec, slots_spec)
    return jax.shard_map(
        functools.partial(on_device, mesh.shape["energy"], mesh.shape["wire"]),
        mesh=mesh, in_specs=in_specs, out_specs=out_specs, check_vma=False,
    )
```

```python
import functools

import jax
import jax.numpy as jnp
from jax import lax
from jax.experimental import pallas as pl
from jax.experimental.pallas import tpu as pltpu
from jax.sharding import PartitionSpec as P

MESH = pl.DeviceIdType.MESH
F32 = jnp.float32
BF16 = jnp.bfloat16


def split(x):
    hi = x.astype(BF16)
    lo = (x - hi.astype(F32)).astype(BF16)
    return hi, lo


def down_rows(row, n):
    tile = jnp.broadcast_to(row, (16, row.shape[1])).astype(BF16)
    return jnp.concatenate([tile] * (n // 16), axis=0)


def dot_nn(a, b):
    return lax.dot_general(a, b, (((1,), (0,)), ((), ())), preferred_element_type=F32)


def dot_nt(a, b):
    return lax.dot_general(a, b, (((1,), (1,)), ((), ())), preferred_element_type=F32)


def dot3(dot, a, b):
    return dot(a[0], b[0]) + (dot(a[1], b[0]) + dot(a[0], b[1]))


def full_one(row):
    n = row.shape[1] // 2
    re, im = row[:, :n], row[:, n:]
    return jnp.concatenate(
        [jnp.concatenate([re, im], axis=1), jnp.concatenate([-im, re], axis=1)], axis=0
    )


def full(row):
    return full_one(row[0]), full_one(row[1])


def sandwich(row, square, state):
    n = row[0].shape[0]
    stacked = state.reshape(2 * n, 2 * n)
    right = dot3(dot_nt, split(stacked), square)
    hi, lo = split(right)
    wide = tuple(
        jnp.concatenate([full_one(x[:n]), full_one(x[n:])], axis=1) for x in (hi, lo)
    )
    out = dot3(dot_nn, row, wide)
    return out[:, : 2 * n], out[:, 2 * n :]


def sandwich_one(row, square, state):
    n = row[0].shape[0]
    right = split(dot3(dot_nt, split(state), square))
    return dot3(dot_nn, row, full(right))


def kernel(
    n_energy, n_wire,
    g_hbm, c_hbm, sl_hbm, sg_hbm, wl_hbm, wg_hbm, pat_hbm, cnt_hbm,
    st, ol_ref, og_ref,
    g, c, sl, sg, wl, wg, pat, cnt_ref,
    acc, pin, lhs, send_w, recv_w, send_g, recv_g, send_s, recv_s,
    in_sem, ring_send, ring_recv, sw_sem, rw_sem, sg_sem, rg_sem, ss_sem, rs_sem,
):
    e = lax.axis_index("energy")
    w = lax.axis_index("wire")
    blocks = g.shape[1]
    n = g.shape[2]
    slots = pat.shape[1]
    part = slots // n_energy
    rows = 4 * blocks

    barrier = pltpu.get_barrier_semaphore()

    def greet(d, carry):
        peer = lax.rem(e + d, n_energy)
        pl.semaphore_signal(barrier, inc=1, device_id={"energy": peer}, device_id_type=MESH)
        return carry

    lax.fori_loop(1, n_energy, greet, 0)

    @pl.when(w > 0)
    def _():
        pl.semaphore_signal(barrier, inc=1, device_id={"wire": w - 1}, device_id_type=MESH)

    @pl.when(w < n_wire - 1)
    def _():
        pl.semaphore_signal(barrier, inc=1, device_id={"wire": w + 1}, device_id_type=MESH)

    pairs = [(pat_hbm, pat), (sl_hbm, sl), (sg_hbm, sg), (wl_hbm, wl), (wg_hbm, wg),
             (g_hbm, g), (c_hbm, c), (cnt_hbm, cnt_ref)]
    loads = [pltpu.make_async_copy(s, d, in_sem.at[i]) for i, (s, d) in enumerate(pairs)]
    for copy in loads:
        copy.start()

    for i in (0, 1, 2, 7):
        loads[i].wait()
    chunk = min(slots, 2048)

    def places(b, off, size):
        p = pat[b : b + 1, pl.ds(off, size)]
        slot = lax.broadcasted_iota(jnp.int32, (1, size), 1) + off
        row = jnp.where(slot < cnt_ref[b], lax.shift_right_logical(p, 7), n)
        col = lax.bitwise_and(p, 127)
        down = lax.broadcasted_iota(jnp.int32, (n, size), 0)
        return down == row, down == col

    acc[...] = jnp.zeros_like(acc)

    def scatter(i, carry):
        off = pl.multiple_of(i * chunk, chunk)
        for b in range(blocks):
            row_is, col_is = places(b, off, chunk)
            hot = jnp.where(col_is, 1.0, 0.0).astype(BF16)
            row_hot = jnp.where(row_is, 1.0, 0.0).astype(BF16)
            his, los = [], []
            for ref in (sl, sg):
                for p in range(2):
                    v = ref[p, b : b + 1, pl.ds(off, chunk)]
                    hi = v.astype(BF16).astype(F32)
                    his.append(row_hot * down_rows(hi, n))
                    los.append(row_hot * down_rows(v - hi, n))
            acc[b] += dot_nt(jnp.concatenate(his + los, axis=0), hot)
        return carry

    lax.fori_loop(0, slots // chunk, scatter, 0)

    loads[5].wait()
    loads[6].wait()
    mults = []
    total = None
    through = None
    for b in range(blocks):
        g_row = split(jnp.concatenate([g[0, b], g[1, b]], axis=1))
        c_row = split(jnp.concatenate([c[0, b], c[1, b]], axis=1))
        mult = split(dot3(dot_nn, g_row, full(c_row)))
        dense = acc[b]
        dense = dense[: 4 * n] + dense[4 * n :]
        less = jnp.concatenate([dense[:n], dense[n : 2 * n]], axis=1)
        greater = jnp.concatenate([dense[2 * n : 3 * n], dense[3 * n :]], axis=1)
        source = sandwich(g_row, full(g_row), jnp.stack([less, greater]))
        if b == 0:
            through = mult
            total = source
        else:
            square = full(mult)
            moved = sandwich(mult, square, st[b - 1])
            total = (source[0] + moved[0], source[1] + moved[1])
            through = split(dot3(dot_nn, mult, full(through)))
        st[b, 0] = total[0]
        st[b, 1] = total[1]
        mults.append(through)

    loads[3].wait()
    loads[4].wait()
    for t in range(n_energy):
        for p in range(2):
            for k, ref in enumerate((wl, wg)):
                for b in range(blocks):
                    row = p * 2 * blocks + k * blocks + b
                    send_w[t, row : row + 1, :] = ref[p, b : b + 1, t * part : (t + 1) * part]
    beside = jnp.where(w > 0, 1, 0) + jnp.where(w < n_wire - 1, 1, 0)
    pl.semaphore_wait(barrier, n_energy - 1 + beside)

    def to_peer(src, dst, s_sem, r_sem, peer):
        return pltpu.make_async_remote_copy(
            src_ref=src.at[peer], dst_ref=dst.at[e], send_sem=s_sem.at[peer],
            recv_sem=r_sem.at[e], device_id={"energy": peer}, device_id_type=MESH)

    def from_peer(src, dst, s_sem, r_sem, peer):
        return pltpu.make_async_remote_copy(
            src_ref=src.at[peer], dst_ref=dst.at[peer], send_sem=s_sem.at[peer],
            recv_sem=r_sem.at[peer], device_id={"energy": peer}, device_id_type=MESH)

    def start_w(d, carry):
        to_peer(send_w, recv_w, sw_sem, rw_sem, lax.rem(e + d, n_energy)).start()
        return carry

    last = blocks - 1

    def ring(k):
        return pltpu.make_async_remote_copy(
            src_ref=st.at[last, k], dst_ref=pin.at[k], send_sem=ring_send.at[k],
            recv_sem=ring_recv.at[k], device_id={"wire": w + 1}, device_id_type=MESH)

    def arrive(k):
        return pltpu.make_async_remote_copy(
            src_ref=st.at[last, k], dst_ref=pin.at[k], send_sem=ring_send.at[k],
            recv_sem=ring_recv.at[k], device_id={"wire": w - 1}, device_id_type=MESH)

    def advance(b, k):
        st[b, k] += sandwich_one(mults[b], full(mults[b]), pin[k])

    @pl.when(w == 0)
    def _():
        for k in range(2):
            ring(k).start()

    lax.fori_loop(1, n_energy, start_w, 0)
    recv_w[e] = send_w[e]
    for k in range(2):

        @pl.when(w > 0)
        def _():
            arrive(k).wait_recv()
            advance(last, k)

        @pl.when(jnp.logical_and(w > 0, w < n_wire - 1))
        def _():
            ring(k).start()

    @pl.when(w > 0)
    def _():
        for b in range(last):
            for k in range(2):
                advance(b, k)

    for b in range(blocks):
        for k in range(2):
            hi, lo = split(st[b, k])
            for p in range(2):
                at = (2 * k + p) * n
                lhs[b, at : at + n, :n] = hi[:, p * n : (p + 1) * n]
                lhs[b, at : at + n, n:] = lo[:, p * n : (p + 1) * n]

    def gather(d, carry):
        t = lax.rem(e + d, n_energy)
        off = pl.multiple_of(t * part, part)
        for b in range(blocks):
            row_is, col_is = places(b, off, part)
            hot = jnp.where(col_is, 1.0, 0.0).astype(BF16)
            taken = dot_nn(lhs[b], jnp.concatenate([hot, hot], axis=0))
            for k in range(2):
                for p in range(2):
                    at = (2 * k + p) * n
                    row = p * 2 * blocks + k * blocks + b
                    picked = jnp.where(row_is, taken[at : at + n], 0.0)
                    send_g[t, row : row + 1, :] = jnp.sum(picked, axis=0, keepdims=True)

        @pl.when(d < n_energy)
        def _():
            to_peer(send_g, recv_g, sg_sem, rg_sem, t).start()

        return carry

    lax.fori_loop(1, n_energy + 1, gather, 0)
    recv_g[e] = send_g[e]

    def land(d, carry):
        peer = lax.rem(e + d, n_energy)
        from_peer(send_w, recv_w, sw_sem, rw_sem, peer).wait_recv()
        from_peer(send_g, recv_g, sg_sem, rg_sem, peer).wait_recv()
        return carry

    lax.fori_loop(1, n_energy, land, 0)

    half = rows // 2
    scale = n_energy ** -0.5
    plain, turned, straight, crossed = [], [], [], []
    for k in range(n_energy):
        x = recv_g[k]
        y = recv_w[k]
        plain.append(x)
        turned.append(jnp.concatenate([x[half:], x[:half]], axis=0))
        straight.append(jnp.concatenate([y[:half], y[:half]], axis=0))
        crossed.append(jnp.concatenate([-y[half:], y[half:]], axis=0))
    for f in range(n_energy):
        total = None
        for k in range(f + 1):
            term = plain[f - k] * straight[k] + turned[f - k] * crossed[k]
            total = term if total is None else total + term
        send_s[f] = jnp.concatenate([-scale * total[half:], scale * total[:half]], axis=0)

        @pl.when(e != f)
        def _():
            to_peer(send_s, recv_s, ss_sem, rs_sem, f).start()

    recv_s[e] = send_s[e]

    def land_s(d, carry):
        peer = lax.rem(e + d, n_energy)
        from_peer(send_s, recv_s, ss_sem, rs_sem, peer).wait_recv()
        return carry

    lax.fori_loop(1, n_energy, land_s, 0)
    for t in range(n_energy):
        for p in range(2):
            for k, ref in enumerate((ol_ref, og_ref)):
                for b in range(blocks):
                    row = p * 2 * blocks + k * blocks + b
                    ref[p, b : b + 1, t * part : (t + 1) * part] = recv_s[t, row : row + 1, :]

    def drain(d, carry):
        peer = lax.rem(e + d, n_energy)
        to_peer(send_w, recv_w, sw_sem, rw_sem, peer).wait_send()
        to_peer(send_g, recv_g, sg_sem, rg_sem, peer).wait_send()
        to_peer(send_s, recv_s, ss_sem, rs_sem, peer).wait_send()
        return carry

    lax.fori_loop(1, n_energy, drain, 0)

    @pl.when(w < n_wire - 1)
    def _():
        ring(0).wait_send()
        ring(1).wait_send()


def hand_over(st, ol, og, gl_hbm, gg_hbm, ol_hbm, og_hbm, sem):
    blocks, n = st.shape[0], st.shape[2]
    pairs = [(ol, ol_hbm), (og, og_hbm)]
    for b in range(blocks):
        for k, dst in enumerate((gl_hbm, gg_hbm)):
            for p in range(2):
                pairs.append((st.at[b, k, :, pl.ds(p * n, n)], dst.at[p, b]))
    copies = [pltpu.make_async_copy(s, d, sem.at[i]) for i, (s, d) in enumerate(pairs)]
    for copy in copies:
        copy.start()
    for copy in copies:
        copy.wait()


def on_device(n_energy, n_wire, green_ret, coupling, sl, sg, wl, wg, pattern, counts):
    blocks, n = green_ret.shape[2], green_ret.shape[3]
    slots = pattern.shape[1]
    part = slots // n_energy
    rows = 4 * blocks
    g = green_ret.reshape(2, blocks, n, n)
    vals = [x.reshape(2, blocks, slots) for x in (sl, sg, wl, wg)]
    hbm_spec = pl.BlockSpec(memory_space=pltpu.HBM)
    vmem_spec = pl.BlockSpec(memory_space=pltpu.VMEM)
    dma = pltpu.SemaphoreType.DMA
    mail = pltpu.VMEM((n_energy, rows, part), F32)
    out = pl.pallas_call(
        functools.partial(kernel, n_energy, n_wire),
        out_shape=[
            pltpu.VMEM((blocks, 2, n, 2 * n), F32),
            pltpu.VMEM((2, blocks, slots), F32),
            pltpu.VMEM((2, blocks, slots), F32),
        ],
        in_specs=[hbm_spec] * 8,
        out_specs=[vmem_spec] * 3,
        scratch_shapes=[
            pltpu.VMEM((2, blocks, n, n), F32),
            pltpu.VMEM((2, blocks, n, n), F32),
            pltpu.VMEM((2, blocks, slots), F32),
            pltpu.VMEM((2, blocks, slots), F32),
            pltpu.VMEM((2, blocks, slots), F32),
            pltpu.VMEM((2, blocks, slots), F32),
            pltpu.VMEM((blocks, slots), jnp.int32),
            pltpu.SMEM((blocks,), jnp.int32),
            pltpu.VMEM((blocks, 8 * n, n), F32),
            pltpu.VMEM((2, n, 2 * n), F32),
            pltpu.VMEM((blocks, 4 * n, 2 * n), BF16),
            mail, mail, mail, mail, mail, mail,
            dma((8,)), dma((2,)), dma((2,)),
            dma((n_energy,)), dma((n_energy,)), dma((n_energy,)),
            dma((n_energy,)), dma((n_energy,)), dma((n_energy,)),
        ],
        compiler_params=pltpu.CompilerParams(
            collective_id=0, has_side_effects=True, vmem_limit_bytes=40 * 1024 * 1024
        ),
    )(*[pltpu.with_memory_space_constraint(x, pltpu.HBM) for x in (g, coupling, *vals, pattern, counts)])
    out = pl.pallas_call(
        hand_over,
        out_shape=[
            jax.ShapeDtypeStruct((2, blocks, n, n), F32),
            jax.ShapeDtypeStruct((2, blocks, n, n), F32),
            jax.ShapeDtypeStruct((2, blocks, slots), F32),
            jax.ShapeDtypeStruct((2, blocks, slots), F32),
        ],
        in_specs=[vmem_spec] * 3,
        out_specs=[hbm_spec] * 4,
        scratch_shapes=[dma((2 + 4 * blocks,))],
    )(*[pltpu.with_memory_space_constraint(x, pltpu.VMEM) for x in out])
    return (
        out[0].reshape(green_ret.shape),
        out[1].reshape(green_ret.shape),
        out[2].reshape(sl.shape),
        out[3].reshape(sl.shape),
    )


def solution(mesh):
    blocks_spec = P(None, "energy", "wire", None, None)
    slots_spec = P(None, "energy", "wire", None)
    in_specs = (
        blocks_spec, P(None, "wire", None, None),
        slots_spec, slots_spec, slots_spec, slots_spec,
        P("wire", None), P("wire"),
    )
    out_specs = (blocks_spec, blocks_spec, slots_spec, slots_spec)
    return jax.shard_map(
        functools.partial(on_device, mesh.shape["energy"], mesh.shape["wire"]),
        mesh=mesh, in_specs=in_specs, out_specs=out_specs, check_vma=False,
    )
```

```python
import functools

import jax
import jax.numpy as jnp
from jax import lax
from jax.experimental import pallas as pl
from jax.experimental.pallas import tpu as pltpu
from jax.sharding import PartitionSpec as P

MESH = pl.DeviceIdType.MESH
F32 = jnp.float32
BF16 = jnp.bfloat16


def split(x):
    hi = x.astype(BF16)
    lo = (x - hi.astype(F32)).astype(BF16)
    return hi, lo


def down_rows(row, n):
    tile = jnp.broadcast_to(row, (16, row.shape[1])).astype(BF16)
    return jnp.concatenate([tile] * (n // 16), axis=0)


def dot_nn(a, b):
    return lax.dot_general(a, b, (((1,), (0,)), ((), ())), preferred_element_type=F32)


def dot_nt(a, b):
    return lax.dot_general(a, b, (((1,), (1,)), ((), ())), preferred_element_type=F32)


def dot3(dot, a, b):
    return dot(a[0], b[0]) + (dot(a[1], b[0]) + dot(a[0], b[1]))


def full_one(row):
    n = row.shape[1] // 2
    re, im = row[:, :n], row[:, n:]
    return jnp.concatenate(
        [jnp.concatenate([re, im], axis=1), jnp.concatenate([-im, re], axis=1)], axis=0
    )


def full(row):
    return full_one(row[0]), full_one(row[1])


def sandwich(row, square, state):
    n = row[0].shape[0]
    stacked = state.reshape(2 * n, 2 * n)
    right = dot3(dot_nt, split(stacked), square)
    hi, lo = split(right)
    wide = tuple(
        jnp.concatenate([full_one(x[:n]), full_one(x[n:])], axis=1) for x in (hi, lo)
    )
    out = dot3(dot_nn, row, wide)
    return out[:, : 2 * n], out[:, 2 * n :]


def sandwich_one(row, square, state):
    n = row[0].shape[0]
    right = split(dot3(dot_nt, split(state), square))
    return dot3(dot_nn, row, full(right))


def kernel(
    n_energy, n_wire,
    g_hbm, c_hbm, sl_hbm, sg_hbm, wl_hbm, wg_hbm, pat_hbm, cnt_hbm,
    st, ol_ref, og_ref,
    g, c, sl, sg, wl, wg, pat, cnt_ref,
    acc, pin, lhs, send_w, recv_w, send_g, recv_g, send_s, recv_s,
    in_sem, ring_send, ring_recv, sw_sem, rw_sem, sg_sem, rg_sem, ss_sem, rs_sem,
):
    e = lax.axis_index("energy")
    w = lax.axis_index("wire")
    blocks = g.shape[1]
    n = g.shape[2]
    slots = pat.shape[1]
    part = slots // n_energy
    rows = 4 * blocks

    barrier = pltpu.get_barrier_semaphore()

    def greet(d, carry):
        peer = lax.rem(e + d, n_energy)
        pl.semaphore_signal(barrier, inc=1, device_id={"energy": peer}, device_id_type=MESH)
        return carry

    lax.fori_loop(1, n_energy, greet, 0)

    @pl.when(w > 0)
    def _():
        pl.semaphore_signal(barrier, inc=1, device_id={"wire": w - 1}, device_id_type=MESH)

    @pl.when(w < n_wire - 1)
    def _():
        pl.semaphore_signal(barrier, inc=1, device_id={"wire": w + 1}, device_id_type=MESH)

    pairs = [(pat_hbm, pat), (sl_hbm, sl), (sg_hbm, sg), (wl_hbm, wl), (wg_hbm, wg),
             (g_hbm, g), (c_hbm, c), (cnt_hbm, cnt_ref)]
    loads = [pltpu.make_async_copy(s, d, in_sem.at[i]) for i, (s, d) in enumerate(pairs)]
    for copy in loads:
        copy.start()

    for i in (0, 1, 2, 7):
        loads[i].wait()
    chunk = min(slots, 2048)

    def places(b, off, size):
        p = pat[b : b + 1, pl.ds(off, size)]
        slot = lax.broadcasted_iota(jnp.int32, (1, size), 1) + off
        row = jnp.where(slot < cnt_ref[b], lax.shift_right_logical(p, 7), n)
        col = lax.bitwise_and(p, 127)
        down = lax.broadcasted_iota(jnp.int32, (n, size), 0)
        return down == row, down == col

    acc[...] = jnp.zeros_like(acc)

    def scatter(i, carry):
        off = pl.multiple_of(i * chunk, chunk)
        for b in range(blocks):
            row_is, col_is = places(b, off, chunk)
            hot = jnp.where(col_is, 1.0, 0.0).astype(BF16)
            row_hot = jnp.where(row_is, 1.0, 0.0).astype(BF16)
            his, los = [], []
            for ref in (sl, sg):
                for p in range(2):
                    v = ref[p, b : b + 1, pl.ds(off, chunk)]
                    hi = v.astype(BF16).astype(F32)
                    his.append(row_hot * down_rows(hi, n))
                    los.append(row_hot * down_rows(v - hi, n))
            acc[b] += dot_nt(jnp.concatenate(his + los, axis=0), hot)
        return carry

    lax.fori_loop(0, slots // chunk, scatter, 0)

    loads[5].wait()
    loads[6].wait()
    mults = []
    total = None
    through = None
    for b in range(blocks):
        g_row = split(jnp.concatenate([g[0, b], g[1, b]], axis=1))
        c_row = split(jnp.concatenate([c[0, b], c[1, b]], axis=1))
        mult = split(dot3(dot_nn, g_row, full(c_row)))
        dense = acc[b]
        dense = dense[: 4 * n] + dense[4 * n :]
        less = jnp.concatenate([dense[:n], dense[n : 2 * n]], axis=1)
        greater = jnp.concatenate([dense[2 * n : 3 * n], dense[3 * n :]], axis=1)
        source = sandwich(g_row, full(g_row), jnp.stack([less, greater]))
        if b == 0:
            through = mult
            total = source
        else:
            square = full(mult)
            moved = sandwich(mult, square, st[b - 1])
            total = (source[0] + moved[0], source[1] + moved[1])
            through = split(dot3(dot_nn, mult, full(through)))
        st[b, 0] = total[0]
        st[b, 1] = total[1]
        mults.append(through)

    loads[3].wait()
    loads[4].wait()
    for t in range(n_energy):
        for p in range(2):
            for k, ref in enumerate((wl, wg)):
                for b in range(blocks):
                    row = p * 2 * blocks + k * blocks + b
                    send_w[t, row : row + 1, :] = ref[p, b : b + 1, t * part : (t + 1) * part]
    beside = jnp.where(w > 0, 1, 0) + jnp.where(w < n_wire - 1, 1, 0)
    pl.semaphore_wait(barrier, n_energy - 1 + beside)

    middle = n_energy // 2

    def far(d):
        if n_energy % 2:
            return d
        return jnp.where(d <= middle, d + middle - 1, d - middle)

    def to_peer(src, dst, s_sem, r_sem, peer):
        return pltpu.make_async_remote_copy(
            src_ref=src.at[peer], dst_ref=dst.at[e], send_sem=s_sem.at[peer],
            recv_sem=r_sem.at[e], device_id={"energy": peer}, device_id_type=MESH)

    def from_peer(src, dst, s_sem, r_sem, peer):
        return pltpu.make_async_remote_copy(
            src_ref=src.at[peer], dst_ref=dst.at[peer], send_sem=s_sem.at[peer],
            recv_sem=r_sem.at[peer], device_id={"energy": peer}, device_id_type=MESH)

    def start_w(d, carry):
        to_peer(send_w, recv_w, sw_sem, rw_sem, lax.rem(e + d, n_energy)).start()
        return carry

    last = blocks - 1

    def ring(k):
        return pltpu.make_async_remote_copy(
            src_ref=st.at[last, k], dst_ref=pin.at[k], send_sem=ring_send.at[k],
            recv_sem=ring_recv.at[k], device_id={"wire": w + 1}, device_id_type=MESH)

    def arrive(k):
        return pltpu.make_async_remote_copy(
            src_ref=st.at[last, k], dst_ref=pin.at[k], send_sem=ring_send.at[k],
            recv_sem=ring_recv.at[k], device_id={"wire": w - 1}, device_id_type=MESH)

    def advance(b, k):
        st[b, k] += sandwich_one(mults[b], full(mults[b]), pin[k])

    @pl.when(w == 0)
    def _():
        for k in range(2):
            ring(k).start()

    lax.fori_loop(1, n_energy, start_w, 0)
    recv_w[e] = send_w[e]
    for k in range(2):

        @pl.when(w > 0)
        def _():
            arrive(k).wait_recv()
            advance(last, k)

        @pl.when(jnp.logical_and(w > 0, w < n_wire - 1))
        def _():
            ring(k).start()

    @pl.when(w > 0)
    def _():
        for b in range(last):
            for k in range(2):
                advance(b, k)

    for b in range(blocks):
        for k in range(2):
            hi, lo = split(st[b, k])
            for p in range(2):
                at = (2 * k + p) * n
                lhs[b, at : at + n, :n] = hi[:, p * n : (p + 1) * n]
                lhs[b, at : at + n, n:] = lo[:, p * n : (p + 1) * n]

    def gather(d, carry):
        t = lax.rem(e + jnp.where(d < n_energy, far(d), 0), n_energy)
        off = pl.multiple_of(t * part, part)
        for b in range(blocks):
            row_is, col_is = places(b, off, part)
            hot = jnp.where(col_is, 1.0, 0.0).astype(BF16)
            taken = dot_nn(lhs[b], jnp.concatenate([hot, hot], axis=0))
            for k in range(2):
                for p in range(2):
                    at = (2 * k + p) * n
                    row = p * 2 * blocks + k * blocks + b
                    picked = jnp.where(row_is, taken[at : at + n], 0.0)
                    send_g[t, row : row + 1, :] = jnp.sum(picked, axis=0, keepdims=True)

        @pl.when(d < n_energy)
        def _():
            to_peer(send_g, recv_g, sg_sem, rg_sem, t).start()

        return carry

    lax.fori_loop(1, n_energy + 1, gather, 0)
    recv_g[e] = send_g[e]

    def land(d, carry):
        peer = lax.rem(e + d, n_energy)
        from_peer(send_w, recv_w, sw_sem, rw_sem, peer).wait_recv()
        from_peer(send_g, recv_g, sg_sem, rg_sem, peer).wait_recv()
        return carry

    lax.fori_loop(1, n_energy, land, 0)

    half = rows // 2
    scale = n_energy ** -0.5
    plain, turned, straight, crossed = [], [], [], []
    for k in range(n_energy):
        x = recv_g[k]
        y = recv_w[k]
        plain.append(x)
        turned.append(jnp.concatenate([x[half:], x[:half]], axis=0))
        straight.append(jnp.concatenate([y[:half], y[:half]], axis=0))
        crossed.append(jnp.concatenate([-y[half:], y[half:]], axis=0))
    for f in range(n_energy):
        total = None
        for k in range(f + 1):
            term = plain[f - k] * straight[k] + turned[f - k] * crossed[k]
            total = term if total is None else total + term
        send_s[f] = jnp.concatenate([-scale * total[half:], scale * total[:half]], axis=0)

    def start_s(d, carry):
        to_peer(send_s, recv_s, ss_sem, rs_sem, lax.rem(e + far(d), n_energy)).start()
        return carry

    lax.fori_loop(1, n_energy, start_s, 0)
    recv_s[e] = send_s[e]

    def land_s(d, carry):
        peer = lax.rem(e + d, n_energy)
        from_peer(send_s, recv_s, ss_sem, rs_sem, peer).wait_recv()
        return carry

    lax.fori_loop(1, n_energy, land_s, 0)
    for t in range(n_energy):
        for p in range(2):
            for k, ref in enumerate((ol_ref, og_ref)):
                for b in range(blocks):
                    row = p * 2 * blocks + k * blocks + b
                    ref[p, b : b + 1, t * part : (t + 1) * part] = recv_s[t, row : row + 1, :]

    def drain(d, carry):
        peer = lax.rem(e + d, n_energy)
        to_peer(send_w, recv_w, sw_sem, rw_sem, peer).wait_send()
        to_peer(send_g, recv_g, sg_sem, rg_sem, peer).wait_send()
        to_peer(send_s, recv_s, ss_sem, rs_sem, peer).wait_send()
        return carry

    lax.fori_loop(1, n_energy, drain, 0)

    @pl.when(w < n_wire - 1)
    def _():
        ring(0).wait_send()
        ring(1).wait_send()


def hand_over(st, ol, og, gl_hbm, gg_hbm, ol_hbm, og_hbm, sem):
    blocks, n = st.shape[0], st.shape[2]
    pairs = [(ol, ol_hbm), (og, og_hbm)]
    for b in range(blocks):
        for k, dst in enumerate((gl_hbm, gg_hbm)):
            for p in range(2):
                pairs.append((st.at[b, k, :, pl.ds(p * n, n)], dst.at[p, b]))
    copies = [pltpu.make_async_copy(s, d, sem.at[i]) for i, (s, d) in enumerate(pairs)]
    for copy in copies:
        copy.start()
    for copy in copies:
        copy.wait()


def on_device(n_energy, n_wire, green_ret, coupling, sl, sg, wl, wg, pattern, counts):
    blocks, n = green_ret.shape[2], green_ret.shape[3]
    slots = pattern.shape[1]
    part = slots // n_energy
    rows = 4 * blocks
    g = green_ret.reshape(2, blocks, n, n)
    vals = [x.reshape(2, blocks, slots) for x in (sl, sg, wl, wg)]
    hbm_spec = pl.BlockSpec(memory_space=pltpu.HBM)
    vmem_spec = pl.BlockSpec(memory_space=pltpu.VMEM)
    dma = pltpu.SemaphoreType.DMA
    mail = pltpu.VMEM((n_energy, rows, part), F32)
    out = pl.pallas_call(
        functools.partial(kernel, n_energy, n_wire),
        out_shape=[
            pltpu.VMEM((blocks, 2, n, 2 * n), F32),
            pltpu.VMEM((2, blocks, slots), F32),
            pltpu.VMEM((2, blocks, slots), F32),
        ],
        in_specs=[hbm_spec] * 8,
        out_specs=[vmem_spec] * 3,
        scratch_shapes=[
            pltpu.VMEM((2, blocks, n, n), F32),
            pltpu.VMEM((2, blocks, n, n), F32),
            pltpu.VMEM((2, blocks, slots), F32),
            pltpu.VMEM((2, blocks, slots), F32),
            pltpu.VMEM((2, blocks, slots), F32),
            pltpu.VMEM((2, blocks, slots), F32),
            pltpu.VMEM((blocks, slots), jnp.int32),
            pltpu.SMEM((blocks,), jnp.int32),
            pltpu.VMEM((blocks, 8 * n, n), F32),
            pltpu.VMEM((2, n, 2 * n), F32),
            pltpu.VMEM((blocks, 4 * n, 2 * n), BF16),
            mail, mail, mail, mail, mail, mail,
            dma((8,)), dma((2,)), dma((2,)),
            dma((n_energy,)), dma((n_energy,)), dma((n_energy,)),
            dma((n_energy,)), dma((n_energy,)), dma((n_energy,)),
        ],
        compiler_params=pltpu.CompilerParams(
            collective_id=0, has_side_effects=True, vmem_limit_bytes=40 * 1024 * 1024
        ),
    )(*[pltpu.with_memory_space_constraint(x, pltpu.HBM) for x in (g, coupling, *vals, pattern, counts)])
    out = pl.pallas_call(
        hand_over,
        out_shape=[
            jax.ShapeDtypeStruct((2, blocks, n, n), F32),
            jax.ShapeDtypeStruct((2, blocks, n, n), F32),
            jax.ShapeDtypeStruct((2, blocks, slots), F32),
            jax.ShapeDtypeStruct((2, blocks, slots), F32),
        ],
        in_specs=[vmem_spec] * 3,
        out_specs=[hbm_spec] * 4,
        scratch_shapes=[dma((2 + 4 * blocks,))],
    )(*[pltpu.with_memory_space_constraint(x, pltpu.VMEM) for x in out])
    return (
        out[0].reshape(green_ret.shape),
        out[1].reshape(green_ret.shape),
        out[2].reshape(sl.shape),
        out[3].reshape(sl.shape),
    )


def solution(mesh):
    blocks_spec = P(None, "energy", "wire", None, None)
    slots_spec = P(None, "energy", "wire", None)
    in_specs = (
        blocks_spec, P(None, "wire", None, None),
        slots_spec, slots_spec, slots_spec, slots_spec,
        P("wire", None), P("wire"),
    )
    out_specs = (blocks_spec, blocks_spec, slots_spec, slots_spec)
    return jax.shard_map(
        functools.partial(on_device, mesh.shape["energy"], mesh.shape["wire"]),
        mesh=mesh, in_specs=in_specs, out_specs=out_specs, check_vma=False,
    )
```
